128 devices in a mesh: rollout: 4 (over y_lo, core), row: 8 (over x, y_hi), col: 4 (over z).
Axes of the slice: x: 4, y: 4 (y_hi: 2, y_lo: 2; y = y_hi * 2 + y_lo), z: 4, core: 2. Of those that a mesh axis runs over, the one named last changes fastest.
Arguments:
- queries: bfloat16 [16384, 4096], P(('rollout', 'row', 'col')), may hold values from -16 to 16
- keys: bfloat16 [16384, 512], P(('rollout', 'row', 'col')), may hold values from -16 to 16
- values: bfloat16 [16384, 512], P(('rollout', 'row', 'col')), may hold values from -6 to 6
- out_grad: bfloat16 [16384, 4096], P(('rollout', 'row', 'col')), may hold values from -12 to 12
- hidden_in: bfloat16 [16384, 8192], P(('rollout', 'col'), 'row'), may hold values from -1.5 to 1.5
- q_weight: bfloat16 [4096, 8192], P('col', 'row'), may hold values from -0.09375 to 0.09375
- lengths: int32 [4, 32], P('rollout'), may hold values from 1 to 256, 4096 in all within a row
- kv_order: int32 [4], replicated, may hold values from 0 to 3, each once
Outputs:
- key_grad: float32 [16384, 512], P(('rollout', 'row', 'col'))
- value_grad: float32 [16384, 512], P(('rollout', 'row', 'col'))
- input_grad: bfloat16 [16384, 8192], P(('rollout', 'col'), 'row')
- weight_grad: float32 [4096, 8192], P(('rollout', 'col'), 'row')
The draws below stay inside these ranges and needn't reach their ends.
Inputs may be any that keep to these rules, and one draw needn't show every extreme that they name: `lengths`: each row lists, for 16 packed rollouts in order, a prompt length and then a response length; a row sums to 4096 and its largest entry is exactly 256. `kv_order`: A permutation of the 4 key-value heads.
All inputs are finite; a program needn't handle non-finite values.
Results may differ from the reference program's by a relative error of at most 0.0057.
Values may be sent and summed in bfloat16 or wider, within the bound.
No kernel may reach another device: no remote copies, remote signals or barrier semaphores. Data moves between devices by JAX's collectives and lax.ppermute only.
A program may use at most 192 MiB of HBM per device.

```python
import math
import jax
import jax.numpy as jnp
import numpy as np
from jax import lax

D = 8192
HQ = 32
KV = 4
HD = 128
ROLLS = 16
GROUPS = 4
TOK_G = 4096
TOKENS = 16384
MOST = 256
N_ROLLOUT = 4


def paired_draw(key):
    query_key = jax.random.fold_in(key, 101)
    key_key = jax.random.fold_in(key, 202)
    query_vals = jnp.clip(jax.random.normal(query_key, (TOKENS, HQ * HD), jnp.float32), -4.0, 4.0)
    key_vals = jnp.clip(jax.random.normal(key_key, (TOKENS, KV * HD), jnp.float32), -4.0, 4.0)
    return (query_vals, key_vals)


def draw_queries(key, part):
    return paired_draw(key)[0].astype(jnp.bfloat16)


def draw_keys(key, part):
    return paired_draw(key)[1].astype(jnp.bfloat16)


def block_scale(key, extent, shards, smallest, high):
    gain, own = 1.0, jax.random.fold_in(key, 6)
    for dim, blocks in shards:
        draws = jnp.exp(jax.random.uniform(jax.random.fold_in(own, dim), (blocks,), jnp.float32, smallest / len(shards), high / len(shards)))
        gain = gain * jnp.repeat(draws, extent[dim] // blocks).reshape([-1 if axis == dim else 1 for axis in range(len(extent))])
    return gain


def profile(amount, total, most, skew):
    loads = [(1 << 20) // math.isqrt(rank ** skew) + 1 for rank in range(2, amount + 1)]
    spare, holding = total - most - (amount - 1), [1] * (amount - 1)
    while spare > 0:
        free = [i for i in range(amount - 1) if holding[i] < most]
        pool, remaining = sum([loads[i] for i in free]), spare
        for i in free:
            extra = min(most - holding[i], max(1, remaining * loads[i] // pool), spare)
            holding[i] = holding[i] + extra
            spare = spare - extra
    return np.array([most] + holding)


def uneven(key, count, total, bound, skew):
    if count == 2:
        one = jax.random.randint(key, (), max(1, total - bound), min(bound, total - 1) + 1)
        return jnp.stack([one, total - one])
    sizes = jnp.asarray(profile(count, total, bound, skew), jnp.int32)
    couples = (count - 1) // 2
    giver, receiver = sizes[1:1 + 2 * couples:2], sizes[2:2 + 2 * couples:2]
    slack = jnp.minimum(giver - 1, bound - receiver)
    shifted = jax.random.randint(jax.random.fold_in(key, 1), (couples,), 0, 1 << 20) % (slack + 1)
    sizes = sizes.at[1:1 + 2 * couples:2].set(giver - shifted).at[2:2 + 2 * couples:2].set(receiver + shifted)
    return sizes[jax.random.permutation(jax.random.fold_in(key, 2), count)]


def gaussian(key, shape, scale, most, cuts=(), held_as=jnp.bfloat16):
    gain = block_scale(key, shape, cuts, -0.22, 0.18) if cuts else 1.0
    values = jax.random.normal(key, shape, jnp.float32) * scale * gain
    return jnp.minimum(jnp.maximum(values, -most), most).astype(held_as)


def setup_inputs(seed: int = 0) -> dict:
    splits = jax.random.split(jax.random.key(seed), 9)
    return {
        "queries": draw_queries(jax.random.fold_in(splits[8], 71), 0),
        "keys": draw_keys(jax.random.fold_in(splits[8], 71), 0),
        "values": gaussian(splits[2], (TOKENS, KV * HD), 1.0, 6.0, ((0, 128),)),
        "out_grad": gaussian(splits[3], (TOKENS, HQ * HD), 2.0, 12.0, ((0, 128),)),
        "hidden_in": gaussian(splits[4], (TOKENS, D), 0.25, 1.5, ((0, 16), (1, 8))),
        "q_weight": gaussian(splits[5], (HQ * HD, D), (HQ * HD) ** -0.5, 0.09375, ((0, 4), (1, 8))),
        "lengths": jax.vmap(lambda own: uneven(own, 2 * ROLLS, TOK_G, MOST, 1))(jax.random.split(splits[6], GROUPS)).reshape((GROUPS, 2 * ROLLS)).astype(jnp.int32),
        "kv_order": jax.random.permutation(splits[7], KV).astype(jnp.int32),
    }


def token_parts(lengths_row, length_total):
    bounds = jnp.cumsum(lengths_row).astype(jnp.int32)
    position = jnp.arange(length_total, dtype=jnp.int32)
    return lax.optimization_barrier(jnp.sum((position[:, None] >= bounds[None, :]).astype(jnp.int32), axis=1)).astype(jnp.int32)

def group_grads(queries, keys, values, out_grad, lengths_row, kv_order):
    scale_factor = 1.0 / math.sqrt(HD)
    parts = token_parts(lengths_row, TOK_G)
    document = parts // 2
    response = (parts % 2).astype(jnp.bfloat16)
    position = jnp.arange(TOK_G, dtype=jnp.int32)
    allowed = (position[None, :] <= position[:, None]) & (document[None, :] == document[:, None])
    masked = out_grad * response[:, None]
    kv_of_head = kv_order[jnp.arange(HQ, dtype=jnp.int32) // (HQ // KV)].astype(jnp.int32)
    query_heads = queries.reshape(TOK_G, HQ, HD).transpose(1, 0, 2)
    grad_heads = masked.reshape(TOK_G, HQ, HD).transpose(1, 0, 2)
    key_heads = jnp.take(keys.reshape(TOK_G, KV, HD).transpose(1, 0, 2), kv_of_head, axis=0)
    value_heads = jnp.take(values.reshape(TOK_G, KV, HD).transpose(1, 0, 2), kv_of_head, axis=0)

    def one_head(operands):
        query_rows, key_rows, value_rows, grad_rows = operands
        raw_scores = jnp.dot(query_rows, key_rows.T, preferred_element_type=jnp.float32) * scale_factor
        raw_scores = jnp.where(allowed, raw_scores, -jnp.inf)
        row_top = lax.optimization_barrier(jnp.max(raw_scores, axis=1, keepdims=True))
        exp_scores = jnp.exp(raw_scores - row_top)
        attention = exp_scores / lax.optimization_barrier(jnp.sum(exp_scores, axis=1, keepdims=True))
        attention_half = attention.astype(jnp.bfloat16)
        grad_value = jnp.dot(attention_half.T, grad_rows, preferred_element_type=jnp.float32)
        grad_attention = jnp.dot(grad_rows, value_rows.T, preferred_element_type=jnp.float32)
        row_delta = lax.optimization_barrier(jnp.sum(attention * grad_attention, axis=1, keepdims=True))
        grad_scores = (attention * (grad_attention - row_delta) * scale_factor).astype(jnp.bfloat16)
        grad_query = jnp.dot(grad_scores, key_rows, preferred_element_type=jnp.float32).astype(jnp.bfloat16)
        grad_key = jnp.dot(grad_scores.T, query_rows, preferred_element_type=jnp.float32)
        return (grad_query, grad_key, grad_value)
    head_query, head_key, head_value = lax.map(one_head, (query_heads, key_heads, value_heads, grad_heads))
    query_grad = head_query.transpose(1, 0, 2).reshape(TOK_G, HQ * HD)
    key_list = []
    value_list = []
    for kv_index in range(KV):
        chosen = (kv_of_head == kv_index)[:, None, None]
        key_list.append(lax.optimization_barrier(jnp.sum(jnp.where(chosen, head_key, jnp.zeros_like(head_key)), axis=0)))
        value_list.append(lax.optimization_barrier(jnp.sum(jnp.where(chosen, head_value, jnp.zeros_like(head_value)), axis=0)))
    key_grad = jnp.stack(key_list, axis=1).reshape(TOK_G, KV * HD)
    value_grad = jnp.stack(value_list, axis=1).reshape(TOK_G, KV * HD)
    return (query_grad, key_grad, value_grad)

def reference(queries, keys, values, out_grad, hidden_in, q_weight, lengths, kv_order):
    key_parts = []
    value_parts = []
    input_parts = []
    weight_grad = jnp.zeros((HQ * HD, D), jnp.float32)
    for rollout_group in range(N_ROLLOUT):
        row_first = rollout_group * TOK_G
        row_last = row_first + TOK_G
        query_grad, key_grad, value_grad = group_grads(queries[row_first:row_last], keys[row_first:row_last], values[row_first:row_last], out_grad[row_first:row_last], lengths[rollout_group], kv_order)
        key_parts.append(key_grad)
        value_parts.append(value_grad)
        input_parts.append(jnp.dot(query_grad, q_weight, preferred_element_type=jnp.float32).astype(jnp.bfloat16))
        weight_grad = weight_grad + jnp.dot(query_grad.T, hidden_in[row_first:row_last], preferred_element_type=jnp.float32)
    return (jnp.concatenate(key_parts, axis=0), jnp.concatenate(value_parts, axis=0), jnp.concatenate(input_parts, axis=0), weight_grad)
```

```python
import functools
import math

import jax
import jax.numpy as jnp
from jax import lax
from jax.experimental import pallas as pl
from jax.experimental.pallas import tpu as pltpu
from jax.sharding import PartitionSpec as P

HQ = 32
KV = 4
HD = 128
ROLLS = 16
BF = jnp.bfloat16
F32 = jnp.float32
SCALE = 1.0 / math.sqrt(HD)
SCALE2 = SCALE * math.log2(math.e)
NEG = -1e30
BACK = 4
TB = 128

NT = (((1,), (1,)), ((), ()))
NN = (((1,), (0,)), ((), ()))


def dot(a, b, dims=NN):
    return lax.dot_general(a, b, dims, preferred_element_type=F32)


def attend_kernel(parity, first, order_ref, block_ref, core_ref, len_ref, *refs):
    q_refs, g_refs = refs[0:4], refs[4:8]
    k_refs, v_refs = refs[8:13], refs[13:18]
    rest = refs[18:]
    if first:
        acc_in = None
        qg_ref, acc_out = rest[0:2]
        bias_ref, resp_ref = rest[2:4]
    else:
        acc_in = rest[0]
        qg_ref, own_ref = rest[1:3]
        back_refs = rest[3:7]
        bias_ref, resp_ref = rest[7:9]
    j = pl.program_id(0)

    @pl.when(j == 0)
    def _():
        base = block_ref[0] * TB
        query_pos = base + lax.broadcasted_iota(jnp.int32, (8, TB), 1)
        start = jnp.zeros((8, TB), jnp.int32)
        part = jnp.zeros((8, TB), jnp.int32)
        bound = jnp.int32(0)
        for k in range(2 * ROLLS):
            bound = bound + len_ref[k]
            passed = query_pos >= bound
            part = part + passed.astype(jnp.int32)
            if k % 2 == 1:
                start = jnp.where(passed, bound, start)
        resp_ref[...] = (part % 2).astype(F32)
        key_pos = base - BACK * TB + lax.broadcasted_iota(jnp.int32, ((BACK + 1) * TB, TB), 0)
        allowed = (key_pos >= start[0:1]) & (key_pos <= query_pos[0:1])
        bias_ref[...] = jnp.where(allowed, 0.0, NEG)

    keys = jnp.concatenate([r[...] for r in k_refs], axis=0)
    vals = jnp.concatenate([r[...] for r in v_refs], axis=0)
    keys_t = keys.T
    bias = bias_ref[...]
    bias = jnp.concatenate([bias, bias], axis=1)
    resp = resp_ref[0:1, :]
    resp = jnp.concatenate([resp, resp], axis=1)
    if first:
        dk = jnp.zeros(((BACK + 1) * TB, HD), F32)
        dv = dk
    else:
        dk = acc_in[0]
        dv = acc_in[1]
    column = ((j + core_ref[0]) % 2) * 8 + (j // 2) * 4
    for pair in range(2):
        query = jnp.concatenate([q_refs[2 * pair][...], q_refs[2 * pair + 1][...]], axis=0)
        grad = jnp.concatenate([g_refs[2 * pair][...], g_refs[2 * pair + 1][...]], axis=0)
        scores = dot(keys, query, NT) + bias
        dprobs = dot(vals, grad, NT)
        top = jnp.max(scores, axis=0, keepdims=True)
        raw = jnp.exp2((scores - top) * SCALE2)
        total = jnp.sum(raw, axis=0, keepdims=True)
        norm = resp / total
        probs = raw * norm
        delta = jnp.sum(probs * dprobs, axis=0, keepdims=True)
        dscores = (raw * (norm * SCALE) * (dprobs - delta)).astype(BF)
        dv = dv + dot(probs.astype(BF), grad)
        dk = dk + dot(dscores, query)
        dq = dot(keys_t, dscores).T.astype(BF)
        for c in range(2):
            at = pl.multiple_of((column + 2 * pair + c) * HD, HD)
            qg_ref[:, pl.ds(at, HD)] = dq[c * TB : (c + 1) * TB]

    if first:
        acc_out[0] = dk
        acc_out[1] = dv
    else:
        for b in range(BACK):
            back_refs[b][0] = dk[b * TB : (b + 1) * TB].astype(BF)
            back_refs[b][1] = dv[b * TB : (b + 1) * TB].astype(BF)
        own_ref[0] = dk[BACK * TB :]
        own_ref[1] = dv[BACK * TB :]


def attend(parity, queries, grads, kv_blocks, order, block, core, lengths, acc):
    first = acc is None

    def head_spec(c):
        return pl.BlockSpec((TB, HD), lambda j, o, *_: (0, 8 * j + 2 * c + parity))

    k_spec = pl.BlockSpec((TB, HD), lambda j, o, *_: (0, o[j]))
    v_spec = pl.BlockSpec((TB, HD), lambda j, o, *_: (0, KV + o[j]))
    wide = (BACK + 1) * TB
    acc_spec = pl.BlockSpec((2, wide, HD), lambda j, o, *_: (0, 0, j))
    qg_spec = pl.BlockSpec((TB, 16 * HD), lambda j, o, *_: (0, 0))
    qg_shape = jax.ShapeDtypeStruct((TB, 16 * HD), BF)
    kv_out = pl.BlockSpec((2, TB, HD), lambda j, o, *_: (0, 0, o[j]))
    in_specs = [head_spec(c) for c in range(4)] * 2 + [k_spec] * 5 + [v_spec] * 5
    args = [queries] * 4 + [grads] * 4 + list(kv_blocks) * 2
    if first:
        out_specs = [qg_spec, acc_spec]
        out_shape = [qg_shape, jax.ShapeDtypeStruct((2, wide, KV * HD), F32)]
    else:
        in_specs = in_specs + [acc_spec]
        args = args + [acc]
        out_specs = [qg_spec] + [kv_out] * (1 + BACK)
        out_shape = (
            [qg_shape]
            + [jax.ShapeDtypeStruct((2, TB, KV * HD), F32)]
            + [jax.ShapeDtypeStruct((2, TB, KV * HD), BF)] * BACK
        )
    return pl.pallas_call(
        functools.partial(attend_kernel, parity, first),
        grid_spec=pltpu.PrefetchScalarGridSpec(
            num_scalar_prefetch=4,
            grid=(KV,),
            in_specs=in_specs,
            out_specs=out_specs,
            scratch_shapes=[pltpu.VMEM((wide, TB), F32), pltpu.VMEM((8, TB), F32)],
        ),
        out_shape=out_shape,
        compiler_params=pltpu.CompilerParams(vmem_limit_bytes=48 << 20),
        cost_estimate=pl.CostEstimate(
            flops=16 * 5 * 2 * wide * TB * HD,
            bytes_accessed=8 << 20,
            transcendentals=16 * wide * TB,
        ),
        name="attend%d" % parity,
    )(order, block, core, lengths, *args)


def reorder_kernel(idx_ref, x_ref, o_ref):
    o_ref[...] = x_ref[...]


def reorder(x, idx):
    n = x.shape[0] // TB
    spec = (TB, x.shape[1])
    return pl.pallas_call(
        reorder_kernel,
        grid_spec=pltpu.PrefetchScalarGridSpec(
            num_scalar_prefetch=1,
            grid=(n,),
            in_specs=[pl.BlockSpec(spec, lambda i, t: (t[i], 0))],
            out_specs=pl.BlockSpec(spec, lambda i, t: (i, 0)),
        ),
        out_shape=jax.ShapeDtypeStruct(x.shape, x.dtype),
        cost_estimate=pl.CostEstimate(flops=0, bytes_accessed=4 << 20, transcendentals=0),
        name="reorder",
    )(idx, x)


def project_kernel(core_ref, arrival_ref, ua_ref, ub_ref, own_ref, other_ref, o_ref, acc_ref):
    step = pl.program_id(0)

    def add(first, second):
        for m in range(4):
            rows = pl.ds(m * 2 * TB, 2 * TB)
            term = dot(ua_ref[rows, :], first[...]) + dot(ub_ref[rows, :], second[...])

            @pl.when(step == 0)
            def _():
                acc_ref[rows, :] = term

            @pl.when(step > 0)
            def _():
                acc_ref[rows, :] += term

    @pl.when(core_ref[0] == 0)
    def _():
        add(own_ref, other_ref)

    @pl.when(core_ref[0] == 1)
    def _():
        add(other_ref, own_ref)

    @pl.when(step == pl.num_programs(0) - 1)
    def _():
        for i in range(acc_ref.shape[0] // TB):
            at = pl.multiple_of(arrival_ref[i] * TB, TB)
            o_ref[pl.ds(at, TB), :] = acc_ref[pl.ds(i * TB, TB), :].astype(BF)


def project(used_a, used_b, w_own, w_other, core, arrival):
    tokens, wide = used_a.shape[0], w_own.shape[1]
    used_spec = pl.BlockSpec((tokens, 4 * TB), lambda i, *_: (0, i))
    w_spec = pl.BlockSpec((4 * TB, wide), lambda i, core, _: (2 * (i % 2) + (core[0] + i // 2) % 2, 0))
    return pl.pallas_call(
        project_kernel,
        grid_spec=pltpu.PrefetchScalarGridSpec(
            num_scalar_prefetch=2,
            grid=(4,),
            in_specs=[used_spec] * 2 + [w_spec] * 2,
            out_specs=pl.BlockSpec((tokens, wide), lambda i, *_: (0, 0)),
            scratch_shapes=[pltpu.VMEM((tokens, wide), F32)],
        ),
        out_shape=jax.ShapeDtypeStruct((tokens, wide), BF),
        compiler_params=pltpu.CompilerParams(vmem_limit_bytes=40 << 20),
        cost_estimate=pl.CostEstimate(
            flops=2 * tokens * wide * 4096, bytes_accessed=18 << 20, transcendentals=0
        ),
        name="project",
    )(core, arrival, used_a, used_b, w_own, w_other)


ROWCOL = ("row", "col")
X_UP = [(r, (r + 2) % 8) for r in range(8)]
X_DOWN = [(r, (r - 2) % 8) for r in range(8)]
Y_SWAP = [(r, r ^ 1) for r in range(8)]
CORE_SWAP = [(r, r ^ 1) for r in range(4)]
ONE_CORE = [[4 * (2 * n + core) + c for n in range(2) for c in range(4)] for core in range(2)]


def shift(n):
    return [(b, b + n) for b in range(32) if 0 <= b + n < 32]


def turn():
    pairs = []
    for x in range(4):
        for y in range(2):
            for z in range(4):
                pairs.append(((2 * x + y) * 4 + z, (2 * ((x + z) % 4) + y) * 4 + x))
    return pairs


TURN = turn()


def tie(x, *others):
    return lax.optimization_barrier((x, *others))[0]


def up(x):
    return lax.ppermute(x, "row", X_UP)


def down(x):
    return lax.ppermute(x, "row", X_DOWN)


def swap_y(x):
    return lax.ppermute(x, "row", Y_SWAP)


def share(t0):
    h = TB // 2
    t1 = up(t0)
    t3 = down(t0)
    y0 = swap_y(t0)
    t2 = jnp.concatenate([up(t1[:h]), down(t3[h:])], axis=0)
    y1 = up(y0)
    y3 = down(y0)

    def rest(*after):
        y2 = swap_y(tie(t2, *after))
        return jnp.concatenate([t0, t3, t2, t1, y0, y3, y2, y1], axis=0)

    return rest


def body(queries, keys, values, out_grad, hidden_in, q_weight, lengths, kv_order):
    row = lax.axis_index("row")
    col = lax.axis_index("col")
    rollout = lax.axis_index("rollout")
    core = rollout % 2
    x, y = row // 2, row % 2
    block = (row * 4 + col).astype(jnp.int32).reshape(1)
    core1 = core.astype(jnp.int32).reshape(1)
    wide = q_weight.shape[1]

    kv = jnp.concatenate([keys, values], axis=1)
    kv_blocks = [lax.ppermute(kv, ROWCOL, shift(n)) for n in (4, 3, 2, 1)] + [kv]

    k = (x - col) % 4
    arrival = jnp.stack(
        [4 * (y ^ s) + (k + n) % 4 for s in range(2) for n in range(4)]
    ).astype(jnp.int32)
    hidden = reorder(hidden_in, arrival)
    block = tie(block, hidden)

    lens = lengths[0]
    qa, acc = attend(0, queries, out_grad, kv_blocks, kv_order, block, core1, lens, None)
    outs = attend(1, queries, out_grad, kv_blocks, kv_order, block, core1, lens, acc)
    qb, own = outs[:2]
    back = outs[2:]

    dims = (((0,), (0,)), ((), ()))

    def send_part(used):
        return dot(used[:, used.shape[1] // 2 :], hidden, dims).astype(BF)

    def lower(used, send):
        half = used.shape[1] // 2
        came = lax.ppermute(send, "rollout", CORE_SWAP)
        return (dot(used[:, :half], hidden, dims) + came.astype(F32)).astype(BF)

    def collect(low):
        return lax.all_to_all(
            low, ("rollout", "col"), 0, 0, axis_index_groups=ONE_CORE, tiled=True
        )

    def sum_rows(got):
        return jnp.sum(got.reshape(8, TB, wide).astype(F32), axis=0)

    turn_a = lax.ppermute(qa, ROWCOL, TURN)
    turn_b = lax.ppermute(tie(qb, turn_a), ROWCOL, TURN)

    mine = lax.dynamic_index_in_dim(q_weight.reshape(4, 2, TB, wide), core, 1, keepdims=False)
    mine = tie(mine.reshape(4 * TB, wide), turn_b)
    w_own = lax.all_gather(mine, "col", axis=0, tiled=True)

    rest_a = share(turn_a)
    rest_b = share(turn_b)
    used_a = rest_a()
    send_a = send_part(used_a)
    low_a = lower(used_a, send_a)
    back = [tie(b, turn_a) for b in back]
    total = own
    for b in range(BACK):
        total = total + lax.ppermute(back[b], ROWCOL, shift(b - BACK)).astype(F32)
    used_b = rest_b(low_a, total)
    got_a = collect(low_a)
    w_own = tie(w_own, used_b)
    w_other = lax.ppermute(w_own, "rollout", CORE_SWAP)
    send_b = send_part(used_b)
    low_b = lower(used_b, send_b)
    got_b = collect(low_b)
    input_grad = project(used_a, used_b, w_own, w_other, core1, arrival)
    got_b = tie(got_b, input_grad)
    weight_grad = jnp.concatenate([sum_rows(got_a), sum_rows(got_b)], axis=0)
    return (total[0], total[1], input_grad, weight_grad)


def solution(mesh):
    placed = (
        P(("rollout", "row", "col"), None),
        P(("rollout", "row", "col"), None),
        P(("rollout", "row", "col"), None),
        P(("rollout", "row", "col"), None),
        P(("rollout", "col"), "row"),
        P("col", "row"),
        P("rollout", None),
        P(),
    )
    return jax.shard_map(
        body,
        mesh=mesh,
        in_specs=placed,
        out_specs=(
            P(("rollout", "row", "col"), None),
            P(("rollout", "row", "col"), None),
            P(("rollout", "col"), "row"),
            P(("rollout", "col"), "row"),
        ),
        check_vma=False,
    )
```

```python
import functools
import math

import jax
import jax.numpy as jnp
from jax import lax
from jax.experimental import pallas as pl
from jax.experimental.pallas import tpu as pltpu
from jax.sharding import PartitionSpec as P

HQ = 32
KV = 4
HD = 128
ROLLS = 16
BF = jnp.bfloat16
F32 = jnp.float32
SCALE = 1.0 / math.sqrt(HD)
SCALE2 = SCALE * math.log2(math.e)
NEG = -1e30
BACK = 4
TB = 128

NT = (((1,), (1,)), ((), ()))
NN = (((1,), (0,)), ((), ()))


def dot(a, b, dims=NN):
    return lax.dot_general(a, b, dims, preferred_element_type=F32)


def attend_kernel(parity, first, order_ref, block_ref, core_ref, len_ref, *refs):
    q_refs, g_refs = refs[0:4], refs[4:8]
    k_refs, v_refs = refs[8:13], refs[13:18]
    rest = refs[18:]
    if first:
        acc_in = None
        qg_ref, acc_out = rest[0:2]
        bias_ref, resp_ref = rest[2:4]
    else:
        acc_in = rest[0]
        qg_ref, own_ref = rest[1:3]
        back_refs = rest[3:7]
        bias_ref, resp_ref = rest[7:9]
    j = pl.program_id(0)

    @pl.when(j == 0)
    def _():
        base = block_ref[0] * TB
        query_pos = base + lax.broadcasted_iota(jnp.int32, (8, TB), 1)
        start = jnp.zeros((8, TB), jnp.int32)
        part = jnp.zeros((8, TB), jnp.int32)
        bound = jnp.int32(0)
        for k in range(2 * ROLLS):
            bound = bound + len_ref[k]
            passed = query_pos >= bound
            part = part + passed.astype(jnp.int32)
            if k % 2 == 1:
                start = jnp.where(passed, bound, start)
        resp_ref[...] = (part % 2).astype(F32)
        key_pos = base - BACK * TB + lax.broadcasted_iota(jnp.int32, ((BACK + 1) * TB, TB), 0)
        allowed = (key_pos >= start[0:1]) & (key_pos <= query_pos[0:1])
        bias_ref[...] = jnp.where(allowed, 0.0, NEG)

    keys = jnp.concatenate([r[...] for r in k_refs], axis=0)
    vals = jnp.concatenate([r[...] for r in v_refs], axis=0)
    keys_t = keys.T
    bias = bias_ref[...]
    bias = jnp.concatenate([bias, bias], axis=1)
    resp = resp_ref[0:1, :]
    resp = jnp.concatenate([resp, resp], axis=1)
    if first:
        dk = jnp.zeros(((BACK + 1) * TB, HD), F32)
        dv = dk
    else:
        dk = acc_in[0]
        dv = acc_in[1]
    column = ((j + core_ref[0]) % 2) * 8 + (j // 2) * 4
    for pair in range(2):
        query = jnp.concatenate([q_refs[2 * pair][...], q_refs[2 * pair + 1][...]], axis=0)
        grad = jnp.concatenate([g_refs[2 * pair][...], g_refs[2 * pair + 1][...]], axis=0)
        scores = dot(keys, query, NT) + bias
        dprobs = dot(vals, grad, NT)
        top = jnp.max(scores, axis=0, keepdims=True)
        raw = jnp.exp2((scores - top) * SCALE2)
        total = jnp.sum(raw, axis=0, keepdims=True)
        norm = resp / total
        probs = raw * norm
        delta = jnp.sum(probs * dprobs, axis=0, keepdims=True)
        dscores = (raw * (norm * SCALE) * (dprobs - delta)).astype(BF)
        dv = dv + dot(probs.astype(BF), grad)
        dk = dk + dot(dscores, query)
        dq = dot(keys_t, dscores).T.astype(BF)
        for c in range(2):
            at = pl.multiple_of((column + 2 * pair + c) * HD, HD)
            qg_ref[:, pl.ds(at, HD)] = dq[c * TB : (c + 1) * TB]

    if first:
        acc_out[0] = dk
        acc_out[1] = dv
    else:
        for b in range(BACK):
            back_refs[b][0] = dk[b * TB : (b + 1) * TB].astype(BF)
            back_refs[b][1] = dv[b * TB : (b + 1) * TB].astype(BF)
        own_ref[0] = dk[BACK * TB :]
        own_ref[1] = dv[BACK * TB :]


def attend(parity, queries, grads, kv_blocks, order, block, core, lengths, acc):
    first = acc is None

    def head_spec(c):
        return pl.BlockSpec((TB, HD), lambda j, o, *_: (0, 8 * j + 2 * c + parity))

    k_spec = pl.BlockSpec((TB, HD), lambda j, o, *_: (0, o[j]))
    v_spec = pl.BlockSpec((TB, HD), lambda j, o, *_: (0, KV + o[j]))
    wide = (BACK + 1) * TB
    acc_spec = pl.BlockSpec((2, wide, HD), lambda j, o, *_: (0, 0, j))
    qg_spec = pl.BlockSpec((TB, 16 * HD), lambda j, o, *_: (0, 0))
    qg_shape = jax.ShapeDtypeStruct((TB, 16 * HD), BF)
    kv_out = pl.BlockSpec((2, TB, HD), lambda j, o, *_: (0, 0, o[j]))
    in_specs = [head_spec(c) for c in range(4)] * 2 + [k_spec] * 5 + [v_spec] * 5
    args = [queries] * 4 + [grads] * 4 + list(kv_blocks) * 2
    if first:
        out_specs = [qg_spec, acc_spec]
        out_shape = [qg_shape, jax.ShapeDtypeStruct((2, wide, KV * HD), F32)]
    else:
        in_specs = in_specs + [acc_spec]
        args = args + [acc]
        out_specs = [qg_spec] + [kv_out] * (1 + BACK)
        out_shape = (
            [qg_shape]
            + [jax.ShapeDtypeStruct((2, TB, KV * HD), F32)]
            + [jax.ShapeDtypeStruct((2, TB, KV * HD), BF)] * BACK
        )
    return pl.pallas_call(
        functools.partial(attend_kernel, parity, first),
        grid_spec=pltpu.PrefetchScalarGridSpec(
            num_scalar_prefetch=4,
            grid=(KV,),
            in_specs=in_specs,
            out_specs=out_specs,
            scratch_shapes=[pltpu.VMEM((wide, TB), F32), pltpu.VMEM((8, TB), F32)],
        ),
        out_shape=out_shape,
        compiler_params=pltpu.CompilerParams(vmem_limit_bytes=48 << 20),
        cost_estimate=pl.CostEstimate(
            flops=16 * 5 * 2 * wide * TB * HD,
            bytes_accessed=8 << 20,
            transcendentals=16 * wide * TB,
        ),
        name="attend%d" % parity,
    )(order, block, core, lengths, *args)


def reorder_kernel(idx_ref, x_ref, o_ref):
    o_ref[...] = x_ref[...]


def reorder(x, idx):
    n = x.shape[0] // TB
    spec = (TB, x.shape[1])
    return pl.pallas_call(
        reorder_kernel,
        grid_spec=pltpu.PrefetchScalarGridSpec(
            num_scalar_prefetch=1,
            grid=(n,),
            in_specs=[pl.BlockSpec(spec, lambda i, t: (t[i], 0))],
            out_specs=pl.BlockSpec(spec, lambda i, t: (i, 0)),
        ),
        out_shape=jax.ShapeDtypeStruct(x.shape, x.dtype),
        cost_estimate=pl.CostEstimate(flops=0, bytes_accessed=4 << 20, transcendentals=0),
        name="reorder",
    )(idx, x)


def weight_kernel(*refs):
    piece_refs, hidden_ref, o_ref = refs[:8], refs[8], refs[9]
    used = jnp.concatenate([r[...] for r in piece_refs], axis=0)
    o_ref[...] = dot(used, hidden_ref[...], (((0,), (0,)), ((), ()))).astype(BF)


def weight_part(pieces, hidden, half):
    features, (tokens, wide) = pieces[0].shape[1] // 2, hidden.shape
    step = 4 * TB
    steps = features // step
    return pl.pallas_call(
        weight_kernel,
        grid=(steps,),
        in_specs=[pl.BlockSpec((TB, step), lambda i: (0, i + half * steps))] * 8
        + [pl.BlockSpec((tokens, wide), lambda i: (0, 0))],
        out_specs=pl.BlockSpec((step, wide), lambda i: (i, 0)),
        out_shape=jax.ShapeDtypeStruct((features, wide), BF),
        compiler_params=pltpu.CompilerParams(vmem_limit_bytes=58 << 20),
        cost_estimate=pl.CostEstimate(
            flops=2 * features * tokens * wide, bytes_accessed=6 << 20, transcendentals=0
        ),
        name="weight_part",
    )(*pieces, hidden)


def project_kernel(core_ref, arrival_ref, *refs):
    a_refs, b_refs = refs[:8], refs[8:16]
    own_ref, other_ref, o_ref, acc_ref = refs[16:]
    step = pl.program_id(0)

    even = core_ref[0] == 0
    first = jnp.where(even, own_ref[...], other_ref[...])
    second = jnp.where(even, other_ref[...], own_ref[...])
    for m in range(2):
        rows = pl.ds(m * 4 * TB, 4 * TB)
        left = jnp.concatenate([r[...] for r in a_refs[4 * m : 4 * m + 4]], axis=0)
        right = jnp.concatenate([r[...] for r in b_refs[4 * m : 4 * m + 4]], axis=0)
        term = dot(left, first) + dot(right, second)

        @pl.when(step == 0)
        def _():
            acc_ref[rows, :] = term

        @pl.when(step > 0)
        def _():
            acc_ref[rows, :] += term

    @pl.when(step == pl.num_programs(0) - 1)
    def _():
        for i in range(acc_ref.shape[0] // TB):
            at = pl.multiple_of(arrival_ref[i] * TB, TB)
            o_ref[pl.ds(at, TB), :] = acc_ref[pl.ds(i * TB, TB), :].astype(BF)


def project(pieces_a, pieces_b, w_own, w_other, core, arrival):
    tokens, wide = 8 * TB, w_own.shape[1]
    piece_spec = pl.BlockSpec((TB, 4 * TB), lambda i, *_: (0, i))
    w_spec = pl.BlockSpec(
        (4 * TB, wide), lambda i, core, _: (2 * (i % 2) + (core[0] + i // 2) % 2, 0)
    )
    return pl.pallas_call(
        project_kernel,
        grid_spec=pltpu.PrefetchScalarGridSpec(
            num_scalar_prefetch=2,
            grid=(4,),
            in_specs=[piece_spec] * 16 + [w_spec] * 2,
            out_specs=pl.BlockSpec((tokens, wide), lambda i, *_: (0, 0)),
            scratch_shapes=[pltpu.VMEM((tokens, wide), F32)],
        ),
        out_shape=jax.ShapeDtypeStruct((tokens, wide), BF),
        compiler_params=pltpu.CompilerParams(vmem_limit_bytes=58 << 20),
        cost_estimate=pl.CostEstimate(
            flops=2 * tokens * wide * 4096, bytes_accessed=18 << 20, transcendentals=0
        ),
        name="project",
    )(core, arrival, *pieces_a, *pieces_b, w_own, w_other)


ROWCOL = ("row", "col")
X_UP = [(r, (r + 2) % 8) for r in range(8)]
X_DOWN = [(r, (r - 2) % 8) for r in range(8)]
Y_SWAP = [(r, r ^ 1) for r in range(8)]
NEAR_SWAP = [(r, r ^ 2) for r in range(4)]
Z_UP = [(c, (c + 1) % 4) for c in range(4)]
Z_DOWN = [(c, (c - 1) % 4) for c in range(4)]
Z_FAR = [(c, (c + 2) % 4) for c in range(4)]
CORE_SWAP = [(r, r ^ 1) for r in range(4)]
ONE_CORE = [[4 * (2 * n + core) + c for n in range(2) for c in range(4)] for core in range(2)]


def shift(n):
    return [(b, b + n) for b in range(32) if 0 <= b + n < 32]


def turn():
    pairs = []
    for x in range(4):
        for y in range(2):
            for z in range(4):
                pairs.append(((2 * x + y) * 4 + z, (2 * ((x + z) % 4) + y) * 4 + x))
    return pairs


TURN = turn()


def tie(x, *others):
    return lax.optimization_barrier((x, *others))[0]


def up(x):
    return lax.ppermute(x, "row", X_UP)


def down(x):
    return lax.ppermute(x, "row", X_DOWN)


def swap_y(x):
    return lax.ppermute(x, "row", Y_SWAP)


def share_first(t0):
    return t0, up(t0), down(t0), swap_y(t0)


def share_rest(stage, far_up, *after):
    t0, t1, t3, y0 = stage
    t2 = up(t1) if far_up else down(t3)
    y1 = up(y0)
    y3 = down(y0)
    y2 = swap_y(tie(t2, *after))
    return t0, t3, t2, t1, y0, y3, y2, y1


def body(queries, keys, values, out_grad, hidden_in, q_weight, lengths, kv_order):
    row = lax.axis_index("row")
    col = lax.axis_index("col")
    rollout = lax.axis_index("rollout")
    core, near = rollout % 2, rollout // 2
    x, y = row // 2, row % 2
    block = (row * 4 + col).astype(jnp.int32).reshape(1)
    core1 = core.astype(jnp.int32).reshape(1)
    wide = q_weight.shape[1]

    kv = jnp.concatenate([keys, values], axis=1)
    kv_blocks = [lax.ppermute(kv, ROWCOL, shift(n)) for n in (4, 3, 2, 1)] + [kv]

    k = (x - col) % 4
    arrival = jnp.stack(
        [4 * (y ^ s) + (k + n) % 4 for s in range(2) for n in range(4)]
    ).astype(jnp.int32)
    hidden = reorder(hidden_in, arrival)
    block = tie(block, hidden)

    lens = lengths[0]
    qa, acc = attend(0, queries, out_grad, kv_blocks, kv_order, block, core1, lens, None)
    outs = attend(1, queries, out_grad, kv_blocks, kv_order, block, core1, lens, acc)
    qb, own = outs[:2]
    back = outs[2:]

    def lower(used):
        send = weight_part(used, hidden, 1)
        came = lax.ppermute(send, "rollout", CORE_SWAP)
        keep = weight_part(used, tie(hidden, send), 0)
        return (keep.astype(F32) + came.astype(F32)).astype(BF)

    def collect_far(low):
        low = low.reshape(2, 4, TB, wide)

        def to_col(n):
            return lax.dynamic_index_in_dim(low, (col + n) % 4, 1, keepdims=False)

        rows = (
            to_col(0).astype(F32)
            + lax.ppermute(to_col(1), "col", Z_UP).astype(F32)
            + lax.ppermute(to_col(3), "col", Z_DOWN).astype(F32)
            + lax.ppermute(to_col(2), "col", Z_FAR).astype(F32)
        )
        other = lax.dynamic_index_in_dim(rows, 1 - near, 0, keepdims=False).astype(BF)
        return lax.dynamic_index_in_dim(rows, near, 0, keepdims=False), lax.ppermute(
            other, "rollout", NEAR_SWAP
        )

    def collect(low):
        return lax.all_to_all(
            low, ("rollout", "col"), 0, 0, axis_index_groups=ONE_CORE, tiled=True
        )

    def sum_rows(got):
        return jnp.sum(got.reshape(8, TB, wide).astype(F32), axis=0)

    turn_a = lax.ppermute(qa, ROWCOL, TURN)
    turn_b = lax.ppermute(tie(qb, turn_a), ROWCOL, TURN)

    mine = lax.dynamic_index_in_dim(q_weight.reshape(4, 2, TB, wide), core, 1, keepdims=False)
    mine = tie(mine.reshape(4 * TB, wide), turn_b)
    w_own = lax.all_gather(mine, "col", axis=0, tiled=True)

    first_a = share_first(turn_a)
    first_b = share_first(turn_b)
    used_a = share_rest(first_a, True, *first_b[1:3])
    low_a = lower(used_a)
    total = own
    for b in range(BACK):
        total = total + lax.ppermute(tie(back[b], turn_a), ROWCOL, shift(b - BACK)).astype(F32)
    used_b = share_rest(first_b, False, low_a, total)
    mine_a, came_a = collect_far(low_a)
    *used_b, w_own, mine_a = lax.optimization_barrier((*used_b, w_own, mine_a))
    w_other = lax.ppermute(w_own, "rollout", CORE_SWAP)
    low_b = lower(used_b)
    got_b = collect(low_b)
    input_grad = project(used_a, used_b, w_own, w_other, core1, arrival)
    got_b = tie(got_b, input_grad)
    came_a = tie(came_a, input_grad)
    weight_grad = jnp.concatenate([mine_a + came_a.astype(F32), sum_rows(got_b)], axis=0)
    return (total[0], total[1], input_grad, weight_grad)


def solution(mesh):
    placed = (
        P(("rollout", "row", "col"), None),
        P(("rollout", "row", "col"), None),
        P(("rollout", "row", "col"), None),
        P(("rollout", "row", "col"), None),
        P(("rollout", "col"), "row"),
        P("col", "row"),
        P("rollout", None),
        P(),
    )
    return jax.shard_map(
        body,
        mesh=mesh,
        in_specs=placed,
        out_specs=(
            P(("rollout", "row", "col"), None),
            P(("rollout", "row", "col"), None),
            P(("rollout", "col"), "row"),
            P(("rollout", "col"), "row"),
        ),
        check_vma=False,
    )
```
